256 devices in a mesh: pair: 16 (over z_hi, y, core), aux: 16 (over x, z_lo).
Axes of the slice: x: 4, y: 4, z: 8 (z_hi: 2, z_lo: 4; z = z_hi * 4 + z_lo), core: 2. Of those that a mesh axis runs over, the one named last changes fastest.
Arguments:
- three_index: float32 [32, 768, 8192], P('pair', None, 'aux'), may hold values from -0.6 to 0.6
- occupied_energy: float32 [32], P('pair'), may hold values from -2 to -0.5
- virtual_energy: float32 [768], replicated, may hold values from 0.2 to 3
- plan: int32 [2, 32], P(None, 'pair'), may hold values from 0 to 1, as said below
Outputs:
- gradient_blocks: float32 [32, 768, 8192], P('pair', None, 'aux')
- virtual_density: float32 [768, 768], P('aux', 'pair')
The draws below stay inside these ranges and needn't reach their ends.
Inputs may be any that keep to these rules, and one draw needn't show every extreme that they name: For block p and round r with q = p XOR 2**r: the row plan[r, p * 2 : (p + 1) * 2] is a permutation of the slots, and plan[r, q * 2 + plan[r, p * 2 + k]] = k, so every orbital is paired with exactly one orbital of block q in each round.
All inputs are finite; a program needn't handle non-finite values.
Results may differ from the reference program's by a relative error of at most 0.0001.
Values sent between devices are 32-bit elements; how exact they have to be, the bound alone decides.
A program may use at most 128 MiB of HBM per device.

```python
import jax
import jax.numpy as jnp
from jax import lax

V = 768
NAUX = 8192
OB = 2
ROUNDS = 2
NOCC = 32


def draw_plan(key, part):
    blocks = NOCC // OB
    tables = []
    for turn_index in range(ROUNDS):
        keys = jax.random.split(jax.random.fold_in(key, 11 + turn_index), blocks)
        orders = jax.vmap(lambda single: jax.random.permutation(single, OB))(keys).astype(jnp.int32)
        indices = jnp.arange(blocks)
        upper_side = indices // 2 ** turn_index % 2
        lower_block = indices - upper_side * 2 ** turn_index
        base = orders[lower_block]
        inverse = jnp.argsort(base, axis=1).astype(jnp.int32)
        table = jnp.where(upper_side[:, None] == 1, inverse, base)
        tables.append(table.reshape(-1))
    return jnp.stack(tables).astype(jnp.int32)


def levels(key, shape, cuts, low, largest):
    level, own = 1.0, jax.random.fold_in(key, 6)
    for position, parts in cuts:
        steps = jnp.exp(jax.random.uniform(jax.random.fold_in(own, position), (parts,), jnp.float32, low / len(cuts), largest / len(cuts)))
        level = level * jnp.repeat(steps, shape[position] // parts).reshape([-1 if axis == position else 1 for axis in range(len(shape))])
    return level


def normal_values(rng, shape, spread, limit, pieces=(), held_as=jnp.bfloat16):
    result = spread * jax.random.normal(rng, shape, jnp.float32)
    if pieces:
        result = result * levels(rng, shape, pieces, -0.22, 0.18)
    return jnp.clip(result, -limit, limit).astype(held_as)


def setup_inputs(seed: int = 0) -> dict:
    seeds = jax.random.split(jax.random.key(seed), 5)
    return {
        "three_index": normal_values(seeds[0], (NOCC, V, NAUX), 0.1, 0.6, ((0, 16), (2, 16)), jnp.float32),
        "occupied_energy": jnp.clip(-2.0 + 1.5 * jax.random.uniform(seeds[1], (NOCC,), jnp.float32) ** levels(seeds[1], (NOCC,), ((0, 16),), -0.2, 0.2), -2.0, -0.5),
        "virtual_energy": jnp.clip(jax.random.uniform(seeds[2], (V,), jnp.float32, 0.2, 3.0), 0.2, 3.0),
        "plan": draw_plan(jax.random.fold_in(seeds[4], 71), 0),
    }


def reference(three_index, occupied_energy, virtual_energy, plan):
    highest = lax.Precision.HIGHEST
    blocks = NOCC // OB
    gradient = jnp.zeros(three_index.shape, jnp.float32)
    density = jnp.zeros((V, V), jnp.float32)
    for turn_index in range(ROUNDS):
        for block_index in range(blocks):
            if (block_index >> turn_index) & 1 == 0:
                partner_block = block_index ^ (1 << turn_index)
                for slot_index in range(OB):
                    own_orbital = block_index * OB + slot_index
                    peer_orbital = (partner_block * OB + plan[turn_index, own_orbital]).astype(jnp.int32)
                    left = three_index[own_orbital]
                    right = lax.dynamic_index_in_dim(three_index, peer_orbital, 0, keepdims=False)
                    peer_energy = lax.dynamic_index_in_dim(occupied_energy, peer_orbital, 0, keepdims=False)
                    integral = jnp.dot(left, right.T, precision=highest, preferred_element_type=jnp.float32)
                    denominator = occupied_energy[own_orbital] + peer_energy - virtual_energy[:, None] - virtual_energy[None, :]
                    amplitude = integral / denominator
                    tilde = 2.0 * amplitude - amplitude.T
                    gradient = gradient.at[own_orbital].add(jnp.dot(tilde, right, precision=highest, preferred_element_type=jnp.float32))
                    gradient = gradient.at[peer_orbital].add(jnp.dot(tilde.T, left, precision=highest, preferred_element_type=jnp.float32))
                    density = density + jnp.dot(amplitude, tilde.T, precision=highest, preferred_element_type=jnp.float32)
                    density = density + jnp.dot(amplitude.T, tilde, precision=highest, preferred_element_type=jnp.float32)
    return gradient, density
```

```python
import functools

import jax
import jax.numpy as jnp
from jax import lax
from jax.experimental import pallas as pl
from jax.experimental.pallas import tpu as pltpu
from jax.sharding import PartitionSpec as P

MESH = pl.DeviceIdType.MESH
F32 = jnp.float32
BF16 = jnp.bfloat16
V = 768
NP = 512
SUB = 48
HALF = SUB // 2
CHUNK = 4 * SUB
TILES = V // CHUNK
NN = (((1,), (0,)), ((), ()))
NT = (((1,), (1,)), ((), ()))


def split(value):
    high = value.astype(BF16)
    return high, (value - high.astype(F32)).astype(BF16)


def dot3(left, right, dims):
    (lh, ll), (rh, rl) = left, right

    def one(x, y):
        return lax.dot_general(x, y, dims, preferred_element_type=F32)

    return one(lh, rh) + (one(lh, rl) + one(ll, rh))


def rows(start, count):
    return pl.ds(pl.multiple_of(start, 8), count)


def kernel(
    b_hbm, occ, plan, virt, grad_hbm, dens_out,
    blk, bh, bl, sendb, peer, ph, plo, part, far_in, dir_in, acc, xsum, z_in, full, th, tl, uh, ul,
    rsend, rrecv, gown, outb, dt, d1, s1, d2, s2, d3,
    ld, ex, far, dirs, accs, zs, agz, agx, rel, ret, dsem, outs,
):
    p = lax.axis_index("pair")
    a = lax.axis_index("aux")
    core = p % 2
    y = (p // 2) % 4
    zh = p // 8
    x = a // 4
    z = a % 4

    def at_aux(xx, zz):
        return (p, (xx % 4) * 4 + zz % 4)

    def at_pair(hh, yy, cc):
        return (hh * 8 + (yy % 4) * 2 + cc, a)

    xdev = (at_aux(x + 1, z), at_aux(x + 3, z))
    chip_mate = at_pair(zh, y, 1 - core)
    y_mate = at_pair(zh, y + 1 - 2 * (y % 2), core)
    load = pltpu.make_async_copy(b_hbm, blk, ld)
    load.start()

    barrier = pltpu.get_barrier_semaphore()
    friends = [xdev[0], xdev[1], chip_mate, at_pair(1 - zh, y, core)]
    friends += [at_aux(x, z + j) for j in (1, 2, 3)]
    friends += [at_pair(zh, y + j, core) for j in (1, 2, 3)]
    for dev in friends:
        pl.semaphore_signal(barrier, inc=1, device_id=dev, device_id_type=MESH)

    def remote(src, dst, sems, index, dev):
        return pltpu.make_async_remote_copy(
            src_ref=src,
            dst_ref=dst,
            send_sem=sems.at[(0,) + index],
            recv_sem=sems.at[(1,) + index],
            device_id=dev,
            device_id_type=MESH,
        )

    sent = []

    def go(*args):
        copy = remote(*args)
        copy.start()
        sent.append(copy)

    def own_slot(r):
        upper = (p // (1 + r)) % 2
        return upper * (1 - plan[r, 0])

    def partner(r):
        return (p + (1 + r) - 2 * (1 + r) * ((p // (1 + r)) % 2), a)

    load.wait()

    def fill(r):
        other = 1 - own_slot(r)
        sendb[r, 0:V, :] = blk[other]
        sendb[r, V : V + 8, :] = jnp.full((8, NP), occ[other], F32)

    def exchange(r):
        go(sendb.at[r], peer.at[r], ex, (r,), partner(r))

    fill(0)
    fill(1)
    pl.semaphore_wait(barrier, len(friends))
    exchange(0)
    first_y = [None]

    def start_y():
        exchange(1)

    def split_own(i, carry):
        at = rows(i * CHUNK, CHUNK)
        for slot in range(2):
            high, low = split(blk[slot, at, :])
            bh[slot, at, :] = high
            bl[slot, at, :] = low
        return carry

    def part_chunk(r, c):
        at = rows((c % 4) * CHUNK, CHUNK)
        o = own_slot(r)
        part[r, at, :] = dot3((bh[o, at, :], bl[o, at, :]), (ph[r], plo[r]), NT)

    order = (1, 2, 3, 0)

    def integral(r):
        remote(sendb.at[r], peer.at[r], ex, (r,), partner(r)).wait_recv()

        def split_peer(i, carry):
            at = rows(i * CHUNK, CHUNK)
            high, low = split(peer[r, at, :])
            ph[r, at, :] = high
            plo[r, at, :] = low
            return carry

        lax.fori_loop(0, TILES, split_peer, 0)
        part_chunk(r, x + 2)
        for j in order:
            k = (z + j) % 4
            base = ((x + 2) % 4) * CHUNK + k * SUB
            for d in range(2):
                go(part.at[r, rows(base + d * HALF, HALF)], far_in.at[r, d, k], far, (r, d, k), xdev[d])
        part_chunk(r, x + 1)
        part_chunk(r, x + 3)
        for j in order:
            k = (z + j) % 4
            for d in range(2):
                base = ((x + 1 + 2 * d) % 4) * CHUNK + k * SUB + (1 - d) * HALF
                go(
                    part.at[r, rows(base, HALF)],
                    dir_in.at[r, d, k, pl.ds((1 - d) * HALF, HALF)],
                    dirs, (r, d, k), xdev[d],
                )
        part_chunk(r, x)

    def reduce(r):
        for j in order:
            k = (z + j) % 4
            for d in range(2):
                remote(far_in.at[r, d, k], far_in.at[r, d, k], far, (r, d, k), xdev[d]).wait_recv()
                base = ((x + 1 + 2 * d) % 4) * CHUNK + k * SUB + d * HALF
                acc[r, d, k] = part[r, rows(base, HALF), :] + far_in[r, d, k]
                go(acc.at[r, d, k], dir_in.at[r, d, k, pl.ds(d * HALF, HALF)], accs, (r, d, k), xdev[d])
        for j in order:
            k = (z + j) % 4
            for d in range(2):
                whole = dir_in.at[r, d, k]
                remote(
                    whole.at[pl.ds((1 - d) * HALF, HALF)], whole.at[pl.ds((1 - d) * HALF, HALF)],
                    dirs, (r, d, k), xdev[d],
                ).wait_recv()
                remote(acc.at[r, d, k], whole.at[pl.ds(d * HALF, HALF)], accs, (r, d, k), xdev[d]).wait_recv()
            xsum[r, k] = part[r, rows(x * CHUNK + k * SUB, SUB), :] + dir_in[r, 0, k] + dir_in[r, 1, k]
            if j:
                go(xsum.at[r, k], z_in.at[r, j - 1], zs, (r, j - 1), at_aux(x, z + j))
        total = xsum[r, z]
        for j in (1, 2, 3):
            remote(z_in.at[r, j - 1], z_in.at[r, j - 1], zs, (r, j - 1), at_aux(x, z + j)).wait_recv()
            total = total + z_in[r, j - 1]
        energy = occ[own_slot(r)] + peer[r, V : V + 1, 0:1]
        mine = rows(a * SUB, SUB)
        lane = lax.broadcasted_iota(jnp.int32, (SUB, V), 1)
        line = lax.broadcasted_iota(jnp.int32, (SUB, V), 0) + a * SUB
        level = jnp.sum(jnp.where(lane == line, virt[...], 0.0), axis=1, keepdims=True)
        full[r, mine, :] = total / ((energy - level) - virt[...])

    def block(r, xx, zz):
        return full.at[r, rows((xx % 4) * CHUNK + (zz % 4) * SUB, SUB)]

    def piece(r, xx, zz, d):
        return full.at[r, rows((xx % 4) * CHUNK + (zz % 4) * SUB + d * HALF, HALF)]

    def gather(r):
        mine = block(r, x, z)
        for d in range(2):
            go(mine, mine, agx, (r, d, z), xdev[d])
        for j in (1, 3, 2):
            go(mine, mine, agz, (r, j - 1), at_aux(x, z + j))
        for j in (1, 3, 2):
            got = block(r, x, z - j + 4)
            remote(got, got, agz, (r, j - 1), at_aux(x, z + j)).wait_recv()
            for d in range(2):
                go(got, got, agx, (r, d, (z - j + 4) % 4), xdev[d])
        for j in (0, 1, 3, 2):
            k = (z - j + 4) % 4
            for d in range(2):
                got = block(r, x + 3 - 2 * d, k)
                remote(got, got, agx, (r, d, k), xdev[d]).wait_recv()
                on = piece(r, x + 3 - 2 * d, k, d)
                go(on, on, rel, (r, d, k), xdev[d])
        for j in (0, 1, 3, 2):
            k = (z - j + 4) % 4
            for d in range(2):
                got = piece(r, x + 2, k, d)
                remote(got, got, rel, (r, d, k), xdev[d]).wait_recv()

    def tildes(r):
        def step(i, carry):
            at = pl.ds(pl.multiple_of(i * 128, 128), 128)
            here = full[r, at, :]
            there = full[r, :, at].T
            th[at, :], tl[at, :] = split(2.0 * here - there)
            uh[at, :], ul[at, :] = split(2.0 * there - here)
            return carry

        lax.fori_loop(0, V // 128, step, 0)

    def give_back(r):
        o = own_slot(r)

        def step(i, carry):
            at = rows(i * CHUNK, CHUNK)
            rsend[r, at, :] = dot3((uh[at, :], ul[at, :]), (bh[o], bl[o]), NN)
            return carry

        for i in range(TILES):
            step(i, 0)
            at = pl.ds(i * CHUNK, CHUNK)
            go(rsend.at[r, at], rrecv.at[r, at], ret, (r, i), partner(r))

    def keep(r):
        def step(i, carry):
            at = rows(i * CHUNK, CHUNK)
            gown[r, at, :] = dot3((th[at, :], tl[at, :]), (ph[r], plo[r]), NN)
            return carry

        lax.fori_loop(0, TILES, step, 0)

    def density(r, first):
        mine = rows(a * SUB, SUB)
        amp = full[r, mine, :]
        amp_t = 2.0 * amp - (th[mine, :].astype(F32) + tl[mine, :].astype(F32))
        pad = jnp.zeros((128 - SUB, V), F32)
        amp = split(jnp.concatenate([amp, pad], axis=0))
        amp_t = split(jnp.concatenate([amp_t, pad], axis=0))

        for i in range(TILES):
            at = pl.ds(i * CHUNK, CHUNK)
            value = dot3((th[at, :], tl[at, :]), amp, NT) + dot3((uh[at, :], ul[at, :]), amp_t, NT)
            value = value.reshape(2, 2, SUB, 128)
            if first:
                dt[2 * i : 2 * i + 2] = value
            else:
                dt[2 * i : 2 * i + 2] = dt[2 * i : 2 * i + 2] + value

    def spread():
        one = remote(dt.at[:, 1 - core], d1, dsem, (0,), chip_mate)
        one.start()
        one.wait_recv()
        s1[...] = dt[:, core] + d1[...]
        two = remote(s1.at[pl.ds(4 * (1 - zh), 4)], d2, dsem, (1,), at_pair(1 - zh, y, core))
        two.start()
        two.wait_recv()
        s2[...] = s1[pl.ds(4 * zh, 4)] + d2[...]
        three = [
            remote(s2.at[(y + j) % 4], d3.at[j - 1], dsem, (1 + j,), at_pair(zh, y + j, core)) for j in (1, 2, 3)
        ]
        for copy in three:
            copy.start()
        total = s2[y]
        for j in (1, 2, 3):
            three[j - 1].wait_recv()
            total = total + d3[j - 1]
        total = jnp.concatenate([total, jnp.zeros((128 - SUB, 128), F32)], axis=0).T
        dens_out[...] = total[0:SUB, 0:SUB]
        sent.extend([one, two] + three)

    early = 1 - core

    def first_round(t):
        return (t + early) % 2 if False else t

    lax.fori_loop(0, TILES, split_own, 0)
    start_y()
    for t in range(2):
        r = first_round(t)
        integral(r)
        reduce(r)
        gather(r)
        tildes(r)
        give_back(r)
        keep(r)
        density(r, t == 0)
    spread()

    o0 = own_slot(0)
    o1 = own_slot(1)
    writes = []
    for i in range(TILES):
        at = pl.ds(i * CHUNK, CHUNK)
        for r in range(2):
            remote(rsend.at[r, at], rrecv.at[r, at], ret, (r, i), partner(r)).wait_recv()
        k0, k1, n0, n1 = gown[0, at, :], gown[1, at, :], rrecv[0, at, :], rrecv[1, at, :]
        outb[0, at, :] = jnp.where(o0 == 0, k0, n0) + jnp.where(o1 == 0, k1, n1)
        outb[1, at, :] = jnp.where(o0 == 0, n0, k0) + jnp.where(o1 == 0, n1, k1)
        copy = pltpu.make_async_copy(outb.at[:, at], grad_hbm.at[:, at], outs.at[i])
        copy.start()
        writes.append(copy)
    for copy in sent:
        copy.wait_send()
    for copy in writes:
        copy.wait()


def body(three_index, occupied_energy, virtual_energy, plan):
    vm = pltpu.VMEM
    dma = pltpu.SemaphoreType.DMA
    return pl.pallas_call(
        kernel,
        out_shape=(
            jax.ShapeDtypeStruct((2, V, NP), F32),
            jax.ShapeDtypeStruct((SUB, SUB), F32),
        ),
        in_specs=[
            pl.BlockSpec(memory_space=pl.ANY),
            pl.BlockSpec(memory_space=pltpu.SMEM),
            pl.BlockSpec(memory_space=pltpu.SMEM),
            pl.BlockSpec(memory_space=pltpu.VMEM),
        ],
        out_specs=(pl.BlockSpec(memory_space=pl.ANY), pl.BlockSpec(memory_space=pltpu.VMEM)),
        scratch_shapes=[
            vm((2, V, NP), F32),
            vm((2, V, NP), BF16),
            vm((2, V, NP), BF16),
            vm((2, V + 8, NP), F32),
            vm((2, V + 8, NP), F32),
            vm((2, V, NP), BF16),
            vm((2, V, NP), BF16),
            vm((2, V, V), F32),
            vm((2, 2, 4, HALF, V), F32),
            vm((2, 2, 4, SUB, V), F32),
            vm((2, 2, 4, HALF, V), F32),
            vm((2, 4, SUB, V), F32),
            vm((2, 3, SUB, V), F32),
            vm((2, V, V), F32),
            vm((V, V), BF16),
            vm((V, V), BF16),
            vm((V, V), BF16),
            vm((V, V), BF16),
            vm((2, V, NP), F32),
            vm((2, V, NP), F32),
            vm((2, V, NP), F32),
            vm((2, V, NP), F32),
            vm((8, 2, SUB, 128), F32),
            vm((8, SUB, 128), F32),
            vm((8, SUB, 128), F32),
            vm((4, SUB, 128), F32),
            vm((4, SUB, 128), F32),
            vm((3, SUB, 128), F32),
            dma,
            dma((2, 2)),
            dma((2, 2, 2, 4)),
            dma((2, 2, 2, 4)),
            dma((2, 2, 2, 4)),
            dma((2, 2, 3)),
            dma((2, 2, 3)),
            dma((2, 2, 2, 4)),
            dma((2, 2, 2, 4)),
            dma((2, 2, TILES)),
            dma((2, 5)),
            dma((TILES,)),
        ],
        compiler_params=pltpu.CompilerParams(
            collective_id=0, has_side_effects=True, vmem_limit_bytes=64000 * 1024
        ),
        name="pairs",
    )(three_index, occupied_energy, plan, virtual_energy.reshape(1, V))


def solution(mesh):
    in_specs = (P("pair", None, "aux"), P("pair"), P(), P(None, "pair"))
    out_specs = (P("pair", None, "aux"), P("aux", "pair"))
    return jax.shard_map(body, mesh=mesh, in_specs=in_specs, out_specs=out_specs, check_vma=False)
```

```python
import functools

import jax
import jax.numpy as jnp
from jax import lax
from jax.experimental import pallas as pl
from jax.experimental.pallas import tpu as pltpu
from jax.sharding import PartitionSpec as P

MESH = pl.DeviceIdType.MESH
F32 = jnp.float32
BF16 = jnp.bfloat16
V = 768
NP = 512
SUB = 48
HALF = SUB // 2
CHUNK = 4 * SUB
TILES = V // CHUNK
NN = (((1,), (0,)), ((), ()))
NT = (((1,), (1,)), ((), ()))


def split(value):
    high = value.astype(BF16)
    return high, (value - high.astype(F32)).astype(BF16)


def dot3(left, right, dims):
    (lh, ll), (rh, rl) = left, right

    def one(x, y):
        return lax.dot_general(x, y, dims, preferred_element_type=F32)

    return one(lh, rh) + (one(lh, rl) + one(ll, rh))


def rows(start, count):
    return pl.ds(pl.multiple_of(start, 8), count)


def kernel(
    b_hbm, occ, plan, virt, grad_hbm, dens_out,
    blk, bh, bl, sendb, peer, ph, plo, part, far_in, dir_in, acc, xsum, z_in, full, th, tl, uh, ul,
    rsend, rrecv, gown, outb, dt, d1, s1, d2, s2, d3,
    ld, ex, far, dirs, accs, zs, agz, agx, rel, ret, dsem, outs,
):
    p = lax.axis_index("pair")
    a = lax.axis_index("aux")
    core = p % 2
    y = (p // 2) % 4
    zh = p // 8
    x = a // 4
    z = a % 4

    def at_aux(xx, zz):
        return (p, (xx % 4) * 4 + zz % 4)

    def at_pair(hh, yy, cc):
        return (hh * 8 + (yy % 4) * 2 + cc, a)

    xdev = (at_aux(x + 1, z), at_aux(x + 3, z))
    chip_mate = at_pair(zh, y, 1 - core)
    y_mate = at_pair(zh, y + 1 - 2 * (y % 2), core)
    load = pltpu.make_async_copy(b_hbm, blk, ld)
    load.start()

    barrier = pltpu.get_barrier_semaphore()
    friends = [xdev[0], xdev[1], chip_mate, at_pair(1 - zh, y, core)]
    friends += [at_aux(x, z + j) for j in (1, 2, 3)]
    friends += [at_pair(zh, y + j, core) for j in (1, 2, 3)]
    for dev in friends:
        pl.semaphore_signal(barrier, inc=1, device_id=dev, device_id_type=MESH)

    def remote(src, dst, sems, index, dev):
        return pltpu.make_async_remote_copy(
            src_ref=src,
            dst_ref=dst,
            send_sem=sems.at[(0,) + index],
            recv_sem=sems.at[(1,) + index],
            device_id=dev,
            device_id_type=MESH,
        )

    sent = []

    def go(*args):
        copy = remote(*args)
        copy.start()
        sent.append(copy)

    def upper(r):
        return core + r * (y % 2 - core)

    def own_slot(r):
        return upper(r) * (1 - plan[r, 0])

    def partner(r):
        return (p + (1 + r) * (1 - 2 * upper(r)), a)

    load.wait()

    def fill(r):
        other = 1 - own_slot(r)
        sendb[r, 0:V, :] = blk[other]
        sendb[r, V : V + 8, :] = jnp.full((8, NP), occ[other], F32)

    def exchange(r):
        remote(sendb.at[r], peer.at[r], ex, (r,), partner(r)).start()

    fill(0)
    fill(1)
    pl.semaphore_wait(barrier, len(friends))

    @pl.when(core == 0)
    def _():
        exchange(1)

    exchange(0)

    def split_own(i, carry):
        at = rows(i * CHUNK, CHUNK)
        for slot in range(2):
            high, low = split(blk[slot, at, :])
            bh[slot, at, :] = high
            bl[slot, at, :] = low
        return carry

    def part_chunk(r, c):
        at = rows((c % 4) * CHUNK, CHUNK)
        o = own_slot(r)
        part[r, at, :] = dot3((bh[o, at, :], bl[o, at, :]), (ph[r], plo[r]), NT)

    order = (1, 2, 3, 0)

    def integral(r):
        remote(sendb.at[r], peer.at[r], ex, (r,), partner(r)).wait_recv()

        def split_peer(i, carry):
            at = rows(i * CHUNK, CHUNK)
            high, low = split(peer[r, at, :])
            ph[r, at, :] = high
            plo[r, at, :] = low
            return carry

        lax.fori_loop(0, TILES, split_peer, 0)
        part_chunk(r, x + 2)
        for j in order:
            k = (z + j) % 4
            base = ((x + 2) % 4) * CHUNK + k * SUB
            for d in range(2):
                go(part.at[r, rows(base + d * HALF, HALF)], far_in.at[r, d, k], far, (r, d, k), xdev[d])
        part_chunk(r, x + 1)
        part_chunk(r, x + 3)
        for j in order:
            k = (z + j) % 4
            for d in range(2):
                base = ((x + 1 + 2 * d) % 4) * CHUNK + k * SUB + (1 - d) * HALF
                go(
                    part.at[r, rows(base, HALF)],
                    dir_in.at[r, d, k, pl.ds((1 - d) * HALF, HALF)],
                    dirs, (r, d, k), xdev[d],
                )
        part_chunk(r, x)

    def pass_on(r):
        for j in order:
            k = (z + j) % 4
            for d in range(2):
                remote(far_in.at[r, d, k], far_in.at[r, d, k], far, (r, d, k), xdev[d]).wait_recv()
                base = ((x + 1 + 2 * d) % 4) * CHUNK + k * SUB + d * HALF
                acc[r, d, k] = part[r, rows(base, HALF), :] + far_in[r, d, k]
                go(acc.at[r, d, k], dir_in.at[r, d, k, pl.ds(d * HALF, HALF)], accs, (r, d, k), xdev[d])

    def across(r):
        for j in order:
            k = (z + j) % 4
            for d in range(2):
                whole = dir_in.at[r, d, k]
                remote(
                    whole.at[pl.ds((1 - d) * HALF, HALF)], whole.at[pl.ds((1 - d) * HALF, HALF)],
                    dirs, (r, d, k), xdev[d],
                ).wait_recv()
                remote(acc.at[r, d, k], whole.at[pl.ds(d * HALF, HALF)], accs, (r, d, k), xdev[d]).wait_recv()
            xsum[r, k] = part[r, rows(x * CHUNK + k * SUB, SUB), :] + dir_in[r, 0, k] + dir_in[r, 1, k]
            if j:
                go(xsum.at[r, k], z_in.at[r, j - 1], zs, (r, j - 1), at_aux(x, z + j))

    def amplitude(r):
        total = xsum[r, z]
        for j in (1, 2, 3):
            remote(z_in.at[r, j - 1], z_in.at[r, j - 1], zs, (r, j - 1), at_aux(x, z + j)).wait_recv()
            total = total + z_in[r, j - 1]
        energy = occ[own_slot(r)] + peer[r, V : V + 1, 0:1]
        mine = rows(a * SUB, SUB)
        lane = lax.broadcasted_iota(jnp.int32, (SUB, V), 1)
        line = lax.broadcasted_iota(jnp.int32, (SUB, V), 0) + a * SUB
        level = jnp.sum(jnp.where(lane == line, virt[...], 0.0), axis=1, keepdims=True)
        full[r, mine, :] = total / ((energy - level) - virt[...])

    def block(r, xx, zz):
        return full.at[r, rows((xx % 4) * CHUNK + (zz % 4) * SUB, SUB)]

    def piece(r, xx, zz, d):
        return full.at[r, rows((xx % 4) * CHUNK + (zz % 4) * SUB + d * HALF, HALF)]

    def gather_z(r):
        mine = block(r, x, z)
        for j in (1, 3, 2):
            go(mine, mine, agz, (r, j - 1), at_aux(x, z + j))

    def gather_x(r):
        mine = block(r, x, z)
        for d in range(2):
            go(mine, mine, agx, (r, d, z), xdev[d])

    def onward(r):
        for j in (1, 3, 2):
            got = block(r, x, z - j + 4)
            remote(got, got, agz, (r, j - 1), at_aux(x, z + j)).wait_recv()
            for d in range(2):
                go(got, got, agx, (r, d, (z - j + 4) % 4), xdev[d])

    def relay(r):
        for j in (0, 1, 3, 2):
            k = (z - j + 4) % 4
            for d in range(2):
                got = block(r, x + 3 - 2 * d, k)
                remote(got, got, agx, (r, d, k), xdev[d]).wait_recv()
                on = piece(r, x + 3 - 2 * d, k, d)
                go(on, on, rel, (r, d, k), xdev[d])

    def arrived(r):
        for j in (0, 1, 3, 2):
            k = (z - j + 4) % 4
            for d in range(2):
                got = piece(r, x + 2, k, d)
                remote(got, got, rel, (r, d, k), xdev[d]).wait_recv()

    def tildes(r):
        def step(i, carry):
            at = pl.ds(pl.multiple_of(i * 128, 128), 128)
            here = full[r, at, :]
            there = full[r, :, at].T
            th[at, :], tl[at, :] = split(2.0 * here - there)
            uh[at, :], ul[at, :] = split(2.0 * there - here)
            return carry

        lax.fori_loop(0, V // 128, step, 0)

    def give_back(r):
        o = own_slot(r)

        def step(i, carry):
            at = rows(i * CHUNK, CHUNK)
            rsend[r, at, :] = dot3((uh[at, :], ul[at, :]), (bh[o], bl[o]), NN)
            return carry

        for i in range(TILES):
            step(i, 0)
            at = pl.ds(i * CHUNK, CHUNK)
            go(rsend.at[r, at], rrecv.at[r, at], ret, (r, i), partner(r))

    def keep(r):
        def step(i, carry):
            at = rows(i * CHUNK, CHUNK)
            gown[r, at, :] = dot3((th[at, :], tl[at, :]), (ph[r], plo[r]), NN)
            return carry

        lax.fori_loop(0, TILES, step, 0)

    def density(r, first=False):
        mine = rows(a * SUB, SUB)
        amp = full[r, mine, :]
        amp_t = 2.0 * amp - (th[mine, :].astype(F32) + tl[mine, :].astype(F32))
        pad = jnp.zeros((128 - SUB, V), F32)
        amp = split(jnp.concatenate([amp, pad], axis=0))
        amp_t = split(jnp.concatenate([amp_t, pad], axis=0))

        for i in range(TILES):
            at = pl.ds(i * CHUNK, CHUNK)
            value = dot3((th[at, :], tl[at, :]), amp, NT) + dot3((uh[at, :], ul[at, :]), amp_t, NT)
            value = value.reshape(2, 2, SUB, 128)
            if first:
                dt[2 * i : 2 * i + 2] = value
            else:
                dt[2 * i : 2 * i + 2] = dt[2 * i : 2 * i + 2] + value

    def spread():
        one = remote(dt.at[:, 1 - core], d1, dsem, (0,), chip_mate)
        one.start()
        one.wait_recv()
        s1[...] = dt[:, core] + d1[...]
        two = remote(s1.at[pl.ds(4 * (1 - zh), 4)], d2, dsem, (1,), at_pair(1 - zh, y, core))
        two.start()
        two.wait_recv()
        s2[...] = s1[pl.ds(4 * zh, 4)] + d2[...]
        three = [
            remote(s2.at[(y + j) % 4], d3.at[j - 1], dsem, (1 + j,), at_pair(zh, y + j, core)) for j in (1, 2, 3)
        ]
        for copy in three:
            copy.start()
        total = s2[y]
        for j in (1, 2, 3):
            three[j - 1].wait_recv()
            total = total + d3[j - 1]
        total = jnp.concatenate([total, jnp.zeros((128 - SUB, 128), F32)], axis=0).T
        dens_out[...] = total[0:SUB, 0:SUB]
        sent.extend([one, two] + three)

    def finish():
        o0 = own_slot(0)
        o1 = own_slot(1)
        writes = []
        for i in range(TILES):
            at = pl.ds(i * CHUNK, CHUNK)
            for r in range(2):
                remote(rsend.at[r, at], rrecv.at[r, at], ret, (r, i), partner(r)).wait_recv()
            k0, k1, n0, n1 = gown[0, at, :], gown[1, at, :], rrecv[0, at, :], rrecv[1, at, :]
            outb[0, at, :] = jnp.where(o0 == 0, k0, n0) + jnp.where(o1 == 0, k1, n1)
            outb[1, at, :] = jnp.where(o0 == 0, n0, k0) + jnp.where(o1 == 0, n1, k1)
            copy = pltpu.make_async_copy(outb.at[:, at], grad_hbm.at[:, at], outs.at[i])
            copy.start()
            writes.append(copy)
        for r in range(2):
            remote(sendb.at[r], peer.at[r], ex, (r,), partner(r)).wait_send()
        for copy in sent:
            copy.wait_send()
        for copy in writes:
            copy.wait()

    lax.fori_loop(0, TILES, split_own, 0)
    integral(0)
    pass_on(0)

    @pl.when(core == 1)
    def _():
        exchange(1)

    across(0)
    amplitude(0)
    gather_z(0)
    before = list(sent)

    @pl.when(core == 0)
    def _():
        sent[:] = before
        integral(1)
        pass_on(1)
        gather_x(0)
        across(1)
        onward(0)
        amplitude(1)
        gather_z(1)
        gather_x(1)
        onward(1)
        relay(1)
        relay(0)
        arrived(1)
        tildes(1)
        give_back(1)
        arrived(0)
        keep(1)
        density(1, True)
        tildes(0)
        give_back(0)
        keep(0)
        density(0)
        spread()
        finish()

    @pl.when(core == 1)
    def _():
        sent[:] = before
        gather_x(0)
        onward(0)
        relay(0)
        integral(1)
        arrived(0)
        pass_on(1)
        tildes(0)
        give_back(0)
        across(1)
        keep(0)
        amplitude(1)
        gather_z(1)
        gather_x(1)
        density(0, True)
        onward(1)
        relay(1)
        arrived(1)
        tildes(1)
        give_back(1)
        keep(1)
        density(1)
        spread()
        finish()


def body(three_index, occupied_energy, virtual_energy, plan):
    vm = pltpu.VMEM
    dma = pltpu.SemaphoreType.DMA
    return pl.pallas_call(
        kernel,
        out_shape=(
            jax.ShapeDtypeStruct((2, V, NP), F32),
            jax.ShapeDtypeStruct((SUB, SUB), F32),
        ),
        in_specs=[
            pl.BlockSpec(memory_space=pl.ANY),
            pl.BlockSpec(memory_space=pltpu.SMEM),
            pl.BlockSpec(memory_space=pltpu.SMEM),
            pl.BlockSpec(memory_space=pltpu.VMEM),
        ],
        out_specs=(pl.BlockSpec(memory_space=pl.ANY), pl.BlockSpec(memory_space=pltpu.VMEM)),
        scratch_shapes=[
            vm((2, V, NP), F32),
            vm((2, V, NP), BF16),
            vm((2, V, NP), BF16),
            vm((2, V + 8, NP), F32),
            vm((2, V + 8, NP), F32),
            vm((2, V, NP), BF16),
            vm((2, V, NP), BF16),
            vm((2, V, V), F32),
            vm((2, 2, 4, HALF, V), F32),
            vm((2, 2, 4, SUB, V), F32),
            vm((2, 2, 4, HALF, V), F32),
            vm((2, 4, SUB, V), F32),
            vm((2, 3, SUB, V), F32),
            vm((2, V, V), F32),
            vm((V, V), BF16),
            vm((V, V), BF16),
            vm((V, V), BF16),
            vm((V, V), BF16),
            vm((2, V, NP), F32),
            vm((2, V, NP), F32),
            vm((2, V, NP), F32),
            vm((2, V, NP), F32),
            vm((8, 2, SUB, 128), F32),
            vm((8, SUB, 128), F32),
            vm((8, SUB, 128), F32),
            vm((4, SUB, 128), F32),
            vm((4, SUB, 128), F32),
            vm((3, SUB, 128), F32),
            dma,
            dma((2, 2)),
            dma((2, 2, 2, 4)),
            dma((2, 2, 2, 4)),
            dma((2, 2, 2, 4)),
            dma((2, 2, 3)),
            dma((2, 2, 3)),
            dma((2, 2, 2, 4)),
            dma((2, 2, 2, 4)),
            dma((2, 2, TILES)),
            dma((2, 5)),
            dma((TILES,)),
        ],
        compiler_params=pltpu.CompilerParams(
            collective_id=0, has_side_effects=True, vmem_limit_bytes=64000 * 1024
        ),
        name="pairs",
    )(three_index, occupied_energy, plan, virtual_energy.reshape(1, V))


def solution(mesh):
    in_specs = (P("pair", None, "aux"), P("pair"), P(), P(None, "pair"))
    out_specs = (P("pair", None, "aux"), P("aux", "pair"))
    return jax.shard_map(body, mesh=mesh, in_specs=in_specs, out_specs=out_specs, check_vma=False)
```

```python
import functools

import jax
import jax.numpy as jnp
from jax import lax
from jax.experimental import pallas as pl
from jax.experimental.pallas import tpu as pltpu
from jax.sharding import PartitionSpec as P

MESH = pl.DeviceIdType.MESH
F32 = jnp.float32
BF16 = jnp.bfloat16
V = 768
NP = 512
SUB = 48
HALF = SUB // 2
CHUNK = 4 * SUB
TILES = V // CHUNK
NN = (((1,), (0,)), ((), ()))
NT = (((1,), (1,)), ((), ()))


def split(value):
    high = value.astype(BF16)
    return high, (value - high.astype(F32)).astype(BF16)


def dot3(left, right, dims):
    (lh, ll), (rh, rl) = left, right

    def one(x, y):
        return lax.dot_general(x, y, dims, preferred_element_type=F32)

    return one(lh, rh) + (one(lh, rl) + one(ll, rh))


def rows(start, count):
    return pl.ds(pl.multiple_of(start, 8), count)


def kernel(
    b_hbm, occ, plan, virt, grad_hbm, dens_out,
    blk, bh, bl, sendb, peer, ph, plo, part, far_in, dir_in, acc, xsum, z_in, full, th, tl, uh, ul,
    rsend, rrecv, gown, dt, d1, s1, d2, s2, d3,
    ld, ex, far, dirs, accs, zs, agc, agd, agx, rel, ret, dsem, outs,
):
    p = lax.axis_index("pair")
    a = lax.axis_index("aux")
    core = p % 2
    y = (p // 2) % 4
    zh = p // 8
    x = a // 4
    z = a % 4

    def at_aux(xx, zz):
        return (p, (xx % 4) * 4 + zz % 4)

    def at_pair(hh, yy, cc):
        return (hh * 8 + (yy % 4) * 2 + cc, a)

    xdev = (at_aux(x + 1, z), at_aux(x + 3, z))
    zdev = (at_aux(x, z + 1), at_aux(x, z + 3))
    ends = (3, 0)
    chip_mate = at_pair(zh, y, 1 - core)
    y_mate = at_pair(zh, y + 1 - 2 * (y % 2), core)
    load = pltpu.make_async_copy(b_hbm, blk, ld)
    load.start()

    barrier = pltpu.get_barrier_semaphore()
    friends = [xdev[0], xdev[1], chip_mate, at_pair(1 - zh, y, core)]
    friends += [at_aux(x, z + j) for j in (1, 2, 3)]
    friends += [at_pair(zh, y + j, core) for j in (1, 2, 3)]
    for dev in friends:
        pl.semaphore_signal(barrier, inc=1, device_id=dev, device_id_type=MESH)

    def remote(src, dst, sems, index, dev):
        return pltpu.make_async_remote_copy(
            src_ref=src,
            dst_ref=dst,
            send_sem=sems.at[(0,) + index],
            recv_sem=sems.at[(1,) + index],
            device_id=dev,
            device_id_type=MESH,
        )

    sent = []

    def go(*args):
        copy = remote(*args)
        copy.start()
        sent.append(copy)

    def upper(r):
        return core + r * (y % 2 - core)

    def own_slot(r):
        return upper(r) * (1 - plan[r, 0])

    def partner(r):
        return (p + (1 + r) * (1 - 2 * upper(r)), a)

    load.wait()

    def fill(r):
        other = 1 - own_slot(r)
        sendb[r, 0:V, :] = blk[other]
        sendb[r, V : V + 8, :] = jnp.full((8, NP), occ[other], F32)

    def exchange(r):
        remote(sendb.at[r], peer.at[r], ex, (r,), partner(r)).start()

    fill(0)
    fill(1)
    pl.semaphore_wait(barrier, len(friends))

    @pl.when(core == 0)
    def _():
        exchange(1)

    exchange(0)

    def split_own(i, carry):
        at = rows(i * CHUNK, CHUNK)
        for slot in range(2):
            high, low = split(blk[slot, at, :])
            bh[slot, at, :] = high
            bl[slot, at, :] = low
        return carry

    def part_chunk(r, c):
        at = rows((c % 4) * CHUNK, CHUNK)
        o = own_slot(r)
        part[r, at, :] = dot3((bh[o, at, :], bl[o, at, :]), (ph[r], plo[r]), NT)

    order = (1, 2, 3, 0)

    def integral(r):
        remote(sendb.at[r], peer.at[r], ex, (r,), partner(r)).wait_recv()

        def split_peer(i, carry):
            at = rows(i * CHUNK, CHUNK)
            high, low = split(peer[r, at, :])
            ph[r, at, :] = high
            plo[r, at, :] = low
            return carry

        lax.fori_loop(0, TILES, split_peer, 0)
        part_chunk(r, x + 2)
        for j in order:
            k = (z + j) % 4
            base = ((x + 2) % 4) * CHUNK + k * SUB
            for d in range(2):
                go(part.at[r, rows(base + d * HALF, HALF)], far_in.at[r, d, k], far, (r, d, k), xdev[d])
        part_chunk(r, x + 1)
        part_chunk(r, x + 3)
        for j in order:
            k = (z + j) % 4
            for d in range(2):
                base = ((x + 1 + 2 * d) % 4) * CHUNK + k * SUB + (1 - d) * HALF
                go(
                    part.at[r, rows(base, HALF)],
                    dir_in.at[r, d, k, pl.ds((1 - d) * HALF, HALF)],
                    dirs, (r, d, k), xdev[d],
                )
        part_chunk(r, x)

    def pass_on(r):
        for j in order:
            k = (z + j) % 4
            for d in range(2):
                remote(far_in.at[r, d, k], far_in.at[r, d, k], far, (r, d, k), xdev[d]).wait_recv()
                base = ((x + 1 + 2 * d) % 4) * CHUNK + k * SUB + d * HALF
                acc[r, d, k] = part[r, rows(base, HALF), :] + far_in[r, d, k]
                go(acc.at[r, d, k], dir_in.at[r, d, k, pl.ds(d * HALF, HALF)], accs, (r, d, k), xdev[d])

    def across(r):
        for j in order:
            k = (z + j) % 4
            for d in range(2):
                whole = dir_in.at[r, d, k]
                remote(
                    whole.at[pl.ds((1 - d) * HALF, HALF)], whole.at[pl.ds((1 - d) * HALF, HALF)],
                    dirs, (r, d, k), xdev[d],
                ).wait_recv()
                remote(acc.at[r, d, k], whole.at[pl.ds(d * HALF, HALF)], accs, (r, d, k), xdev[d]).wait_recv()
            xsum[r, k] = part[r, rows(x * CHUNK + k * SUB, SUB), :] + dir_in[r, 0, k] + dir_in[r, 1, k]
            if j:
                go(xsum.at[r, k], z_in.at[r, j - 1], zs, (r, j - 1), at_aux(x, z + j))

    def amplitude(r):
        total = xsum[r, z]
        for j in (1, 2, 3):
            remote(z_in.at[r, j - 1], z_in.at[r, j - 1], zs, (r, j - 1), at_aux(x, z + j)).wait_recv()
            total = total + z_in[r, j - 1]
        energy = occ[own_slot(r)] + peer[r, V : V + 1, 0:1]
        mine = rows(a * SUB, SUB)
        lane = lax.broadcasted_iota(jnp.int32, (SUB, V), 1)
        line = lax.broadcasted_iota(jnp.int32, (SUB, V), 0) + a * SUB
        across_v = virt[...].reshape(1, V)
        level = jnp.sum(jnp.where(lane == line, across_v, 0.0), axis=1, keepdims=True)
        full[r, mine, :] = total / ((energy - level) - across_v)

    def block(r, xx, zz):
        return full.at[r, rows((xx % 4) * CHUNK + (zz % 4) * SUB, SUB)]

    def piece(r, xx, zz, d):
        return full.at[r, rows((xx % 4) * CHUNK + (zz % 4) * SUB + d * HALF, HALF)]

    def ring_block(r, d, k):
        return remote(block(r, x, k), block(r, x, k), agx, (r, d, k), xdev[d])

    def straight(r, j):
        mine = block(r, x, z)
        return remote(mine, mine, agd, (r, j - 1), at_aux(x, z + j))

    def gather_z(r):
        for j in (1, 3, 2):
            straight(r, j).start()

    def gather_x(r):
        for d in range(2):
            ring_block(r, d, z).start()

    def onward(r, *which):
        for i in which:
            k = (z - i + 4) % 4
            got = block(r, x, k)
            remote(got, got, agd, (r, i - 1), at_aux(x, z + i)).wait_recv()
            for e in range(2):
                ring_block(r, e, k).start()

    def ring_relay(r, d, k):
        on = piece(r, x + 3 - 2 * d, k, d)
        return remote(on, on, rel, (r, d, k), xdev[d])

    def relay(r, *which):
        for i in which:
            k = (z - i + 4) % 4
            for d in range(2):
                got = block(r, x + 3 - 2 * d, k)
                remote(got, got, agx, (r, d, k), xdev[d]).wait_recv()
                ring_relay(r, d, k).start()

    def column(d, k, xx):
        return remote(block(0, xx, k), block(0, xx, k), agc, (d, k, xx), zdev[d])

    def ring_first():
        for d in range(2):
            got = piece(0, x + 2, z, d)
            remote(got, got, rel, (0, d, z), xdev[d]).wait_recv()
        for d in range(2):
            @pl.when(z != ends[d])
            def _(d=d):
                for xx in range(4):
                    column(d, z, xx).start()

    def hop(*which):
        for i in which:
            for d in range(2):
                k = z - i * (1 - 2 * d)

                @pl.when((k >= 0) & (k <= 3))
                def _(d=d, k=k):
                    for xx in range(4):
                        column(d, k, xx).wait_recv()

                        @pl.when(z != ends[d])
                        def _():
                            column(d, k, xx).start()

    def arrived(r):
        for j in (0, 1, 3, 2):
            k = (z - j + 4) % 4
            for d in range(2):
                got = piece(r, x + 2, k, d)
                remote(got, got, rel, (r, d, k), xdev[d]).wait_recv()

    def tildes(r):
        def step(i, carry):
            at = pl.ds(pl.multiple_of(i * 128, 128), 128)
            here = full[r, at, :]
            there = full[r, :, at].T
            th[at, :], tl[at, :] = split(2.0 * here - there)
            uh[at, :], ul[at, :] = split(2.0 * there - here)
            return carry

        lax.fori_loop(0, V // 128, step, 0)

    def give_back(r, first=0, last=TILES):
        o = own_slot(r)
        for i in range(first, last):
            at = pl.ds(i * CHUNK, CHUNK)
            rsend[r, at, :] = dot3((uh[at, :], ul[at, :]), (bh[o], bl[o]), NN)
            go(rsend.at[r, at], rrecv.at[r, at], ret, (r, i), partner(r))

    def keep(r):
        def step(i, carry):
            at = rows(i * CHUNK, CHUNK)
            gown[r, at, :] = dot3((th[at, :], tl[at, :]), (ph[r], plo[r]), NN)
            return carry

        lax.fori_loop(0, TILES, step, 0)

    def density(r, first=False):
        mine = rows(a * SUB, SUB)
        amp = full[r, mine, :]
        amp_t = 2.0 * amp - (th[mine, :].astype(F32) + tl[mine, :].astype(F32))
        pad = jnp.zeros((128 - SUB, V), F32)
        amp = split(jnp.concatenate([amp, pad], axis=0))
        amp_t = split(jnp.concatenate([amp_t, pad], axis=0))

        for i in range(TILES):
            at = pl.ds(i * CHUNK, CHUNK)
            value = dot3((th[at, :], tl[at, :]), amp, NT) + dot3((uh[at, :], ul[at, :]), amp_t, NT)
            value = value.reshape(2, 2, SUB, 128)
            if first:
                dt[2 * i : 2 * i + 2] = value
            else:
                dt[2 * i : 2 * i + 2] = dt[2 * i : 2 * i + 2] + value

    def column_copies():
        return [remote(s2.at[(y + j) % 4], d3.at[j - 1], dsem, (1 + j,), at_pair(zh, y + j, core)) for j in (1, 2, 3)]

    def chip_copy():
        return remote(dt.at[:, 1 - core], d1, dsem, (0,), chip_mate)

    def far_copy():
        return remote(s1.at[pl.ds(4 * (1 - zh), 4)], d2, dsem, (1,), at_pair(1 - zh, y, core))

    def spread(stage):
        if stage == 0:
            chip_copy().start()
        if stage == 1:
            chip_copy().wait_recv()
            s1[...] = dt[:, core] + d1[...]
            far_copy().start()
        if stage == 2:
            far_copy().wait_recv()
            s2[...] = s1[pl.ds(4 * zh, 4)] + d2[...]
            for copy in column_copies():
                copy.start()

    def settle():
        total = s2[y]
        for j, copy in enumerate(column_copies()):
            copy.wait_recv()
            total = total + d3[j]
        total = jnp.concatenate([total, jnp.zeros((128 - SUB, 128), F32)], axis=0).T
        dens_out[...] = total[0:SUB, 0:SUB]
        sent.extend([chip_copy(), far_copy()] + column_copies())

    def finish(columns):
        o0 = own_slot(0)
        o1 = own_slot(1)
        writes = []
        for i in range(TILES):
            at = pl.ds(i * CHUNK, CHUNK)
            for r in range(2):
                remote(rsend.at[r, at], rrecv.at[r, at], ret, (r, i), partner(r)).wait_recv()
            k0, k1, n0, n1 = gown[0, at, :], gown[1, at, :], rrecv[0, at, :], rrecv[1, at, :]
            gown[0, at, :] = jnp.where(o0 == 0, k0, n0) + jnp.where(o1 == 0, k1, n1)
            gown[1, at, :] = jnp.where(o0 == 0, n0, k0) + jnp.where(o1 == 0, n1, k1)
            copy = pltpu.make_async_copy(gown.at[:, at], grad_hbm.at[:, at], outs.at[i])
            copy.start()
            writes.append(copy)
            if i == 0:
                spread(2)
        settle()
        for r in range(2):
            remote(sendb.at[r], peer.at[r], ex, (r,), partner(r)).wait_send()
        for copy in sent:
            copy.wait_send()
        for r in range(2):
            if r == 0 and columns:
                continue
            for j in (1, 2, 3):
                straight(r, j).wait_send()
            for k in range(4):
                for d in range(2):
                    ring_block(r, d, k).wait_send()
                    ring_relay(r, d, k).wait_send()
        if columns:
            for d in range(2):
                ring_block(0, d, z).wait_send()
                ring_relay(0, d, z).wait_send()
                for k in range(4):
                    @pl.when(((z - k) * (1 - 2 * d) >= 0) & (z != ends[d]))
                    def _(d=d, k=k):
                        for xx in range(4):
                            column(d, k, xx).wait_send()
        for copy in writes:
            copy.wait()

    lax.fori_loop(0, TILES, split_own, 0)
    integral(0)
    pass_on(0)
    before = list(sent)

    @pl.when(core == 0)
    def _():
        sent[:] = before
        integral(1)
        across(0)
        pass_on(1)
        across(1)
        amplitude(1)
        gather_z(1)
        gather_x(1)
        amplitude(0)
        onward(1, 1)
        relay(1, 0)
        onward(1, 3)
        relay(1, 1)
        onward(1, 2)
        relay(1, 3)
        relay(1, 2)
        arrived(1)
        gather_z(0)
        tildes(1)
        give_back(1)
        keep(1)
        density(1, True)
        gather_x(0)
        onward(0, 1, 3, 2)
        relay(0, 0)
        relay(0, 1)
        relay(0, 3, 2)
        arrived(0)
        tildes(0)
        density(0)
        spread(0)
        give_back(0)
        keep(0)
        spread(1)
        finish(False)

    @pl.when(core == 1)
    def _():
        sent[:] = before
        exchange(1)
        across(0)
        amplitude(0)
        gather_x(0)
        integral(1)
        relay(0, 0)
        pass_on(1)
        across(1)
        amplitude(1)
        gather_z(1)
        gather_x(1)
        onward(1, 1)
        relay(1, 0)
        onward(1, 3)
        relay(1, 1)
        onward(1, 2)
        ring_first()
        relay(1, 3)
        relay(1, 2)
        arrived(1)
        tildes(1)
        give_back(1)
        hop(1)
        keep(1)
        hop(2)
        density(1, True)
        hop(3)
        tildes(0)
        density(0)
        spread(0)
        give_back(0)
        keep(0)
        spread(1)
        finish(True)


def body(three_index, occupied_energy, virtual_energy, plan):
    vm = pltpu.VMEM
    dma = pltpu.SemaphoreType.DMA
    return pl.pallas_call(
        kernel,
        out_shape=(
            jax.ShapeDtypeStruct((2, V, NP), F32),
            jax.ShapeDtypeStruct((SUB, SUB), F32),
        ),
        in_specs=[
            pl.BlockSpec(memory_space=pl.ANY),
            pl.BlockSpec(memory_space=pltpu.SMEM),
            pl.BlockSpec(memory_space=pltpu.SMEM),
            pl.BlockSpec(memory_space=pltpu.VMEM),
        ],
        out_specs=(pl.BlockSpec(memory_space=pl.ANY), pl.BlockSpec(memory_space=pltpu.VMEM)),
        scratch_shapes=[
            vm((2, V, NP), F32),
            vm((2, V, NP), BF16),
            vm((2, V, NP), BF16),
            vm((2, V + 8, NP), F32),
            vm((2, V + 8, NP), F32),
            vm((2, V, NP), BF16),
            vm((2, V, NP), BF16),
            vm((2, V, V), F32),
            vm((2, 2, 4, HALF, V), F32),
            vm((2, 2, 4, SUB, V), F32),
            vm((2, 2, 4, HALF, V), F32),
            vm((2, 4, SUB, V), F32),
            vm((2, 3, SUB, V), F32),
            vm((2, V, V), F32),
            vm((V, V), BF16),
            vm((V, V), BF16),
            vm((V, V), BF16),
            vm((V, V), BF16),
            vm((2, V, NP), F32),
            vm((2, V, NP), F32),
            vm((2, V, NP), F32),
            vm((8, 2, SUB, 128), F32),
            vm((8, SUB, 128), F32),
            vm((8, SUB, 128), F32),
            vm((4, SUB, 128), F32),
            vm((4, SUB, 128), F32),
            vm((3, SUB, 128), F32),
            dma,
            dma((2, 2)),
            dma((2, 2, 2, 4)),
            dma((2, 2, 2, 4)),
            dma((2, 2, 2, 4)),
            dma((2, 2, 3)),
            dma((2, 2, 4, 4)),
            dma((2, 2, 3)),
            dma((2, 2, 2, 4)),
            dma((2, 2, 2, 4)),
            dma((2, 2, TILES)),
            dma((2, 5)),
            dma((TILES,)),
        ],
        compiler_params=pltpu.CompilerParams(
            collective_id=0, has_side_effects=True, vmem_limit_bytes=50 * 1024 * 1024
        ),
        name="pairs",
    )(three_index, occupied_energy, plan, virtual_energy)


def solution(mesh):
    in_specs = (P("pair", None, "aux"), P("pair"), P(), P(None, "pair"))
    out_specs = (P("pair", None, "aux"), P("aux", "pair"))
    return jax.shard_map(body, mesh=mesh, in_specs=in_specs, out_specs=out_specs, check_vma=False)
```

```python
import functools

import jax
import jax.numpy as jnp
from jax import lax
from jax.experimental import pallas as pl
from jax.experimental.pallas import tpu as pltpu
from jax.sharding import PartitionSpec as P

MESH = pl.DeviceIdType.MESH
F32 = jnp.float32
BF16 = jnp.bfloat16
V = 768
NP = 512
SUB = 48
HALF = SUB // 2
CHUNK = 4 * SUB
TILES = V // CHUNK
NN = (((1,), (0,)), ((), ()))
NT = (((1,), (1,)), ((), ()))


def split(value):
    high = value.astype(BF16)
    return high, (value - high.astype(F32)).astype(BF16)


def dot3(left, right, dims):
    (lh, ll), (rh, rl) = left, right

    def one(x, y):
        return lax.dot_general(x, y, dims, preferred_element_type=F32)

    return one(lh, rh) + (one(lh, rl) + one(ll, rh))


def rows(start, count):
    return pl.ds(pl.multiple_of(start, 8), count)


def kernel(
    b_hbm, occ, plan, virt, grad_hbm, dens_out,
    blk, bh, bl, sendb, peer, ph, plo, part, far_in, dir_in, acc, xsum, z_in, full, th, tl, uh, ul,
    rsend, rrecv, gown, dt, d1, s1, d2, s2, d3,
    ld, ex, far, dirs, accs, zs, agd, agx, rel, ret, dsem, outs,
):
    p = lax.axis_index("pair")
    a = lax.axis_index("aux")
    core = p % 2
    y = (p // 2) % 4
    zh = p // 8
    x = a // 4
    z = a % 4

    def at_aux(xx, zz):
        return (p, (xx % 4) * 4 + zz % 4)

    def at_pair(hh, yy, cc):
        return (hh * 8 + (yy % 4) * 2 + cc, a)

    xdev = (at_aux(x + 1, z), at_aux(x + 3, z))
    chip_mate = at_pair(zh, y, 1 - core)
    y_mate = at_pair(zh, y + 1 - 2 * (y % 2), core)
    load = pltpu.make_async_copy(b_hbm, blk, ld)
    load.start()

    barrier = pltpu.get_barrier_semaphore()
    friends = [xdev[0], xdev[1], chip_mate, at_pair(1 - zh, y, core)]
    friends += [at_aux(x, z + j) for j in (1, 2, 3)]
    friends += [at_pair(zh, y + j, core) for j in (1, 2, 3)]
    for dev in friends:
        pl.semaphore_signal(barrier, inc=1, device_id=dev, device_id_type=MESH)

    def remote(src, dst, sems, index, dev):
        return pltpu.make_async_remote_copy(
            src_ref=src,
            dst_ref=dst,
            send_sem=sems.at[(0,) + index],
            recv_sem=sems.at[(1,) + index],
            device_id=dev,
            device_id_type=MESH,
        )

    sent = []

    def go(*args):
        copy = remote(*args)
        copy.start()
        sent.append(copy)

    def upper(r):
        return core + r * (y % 2 - core)

    def own_slot(r):
        return upper(r) * (1 - plan[r, 0])

    def partner(r):
        return (p + (1 + r) * (1 - 2 * upper(r)), a)

    load.wait()

    def fill(r):
        other = 1 - own_slot(r)
        sendb[r, 0:V, :] = blk[other]
        sendb[r, V : V + 8, :] = jnp.full((8, NP), occ[other], F32)

    chunks = (2, 1, 3, 0)

    def row_chunk(r, i):
        at = rows(((x + chunks[i]) % 4) * CHUNK, CHUNK) if i < 4 else pl.ds(V, 8)
        return remote(sendb.at[r, at], peer.at[r, at], ex, (r, i), partner(r))

    def exchange(r):
        for i in (4, 0, 1, 2, 3):
            row_chunk(r, i).start()

    fill(0)
    fill(1)
    pl.semaphore_wait(barrier, len(friends))

    @pl.when(core == 0)
    def _():
        exchange(1)

    exchange(0)

    def split_own(i, carry):
        at = rows(i * CHUNK, CHUNK)
        for slot in range(2):
            high, low = split(blk[slot, at, :])
            bh[slot, at, :] = high
            bl[slot, at, :] = low
        return carry

    order = (2, 3, 1, 0)

    def integral(r, *which):
        for i in which:
            if i == 0:
                row_chunk(r, 4).wait_recv()
            row_chunk(r, i).wait_recv()
            c = (x + chunks[i]) % 4
            at = rows(c * CHUNK, CHUNK)
            o = own_slot(r)
            high, low = split(peer[r, at, :])
            ph[r, at, :] = high
            plo[r, at, :] = low
            part[r, at, :] = dot3((high, low), (bh[o], bl[o]), NT)
            for j in order:
                k = (z + j) % 4
                base = c * CHUNK + k * SUB
                if i == 0:
                    for d in range(2):
                        go(part.at[r, rows(base + d * HALF, HALF)], far_in.at[r, d, k], far, (r, d, k), xdev[d])
                elif i < 3:
                    d = i - 1
                    go(
                        part.at[r, rows(base + (1 - d) * HALF, HALF)],
                        dir_in.at[r, d, k, pl.ds((1 - d) * HALF, HALF)],
                        dirs, (r, d, k), xdev[d],
                    )

    def pass_on(r):
        for j in order:
            k = (z + j) % 4
            for d in range(2):
                remote(far_in.at[r, d, k], far_in.at[r, d, k], far, (r, d, k), xdev[d]).wait_recv()
                base = ((x + 1 + 2 * d) % 4) * CHUNK + k * SUB + d * HALF
                acc[r, d, k] = part[r, rows(base, HALF), :] + far_in[r, d, k]
                go(acc.at[r, d, k], dir_in.at[r, d, k, pl.ds(d * HALF, HALF)], accs, (r, d, k), xdev[d])

    def across(r):
        for j in order:
            k = (z + j) % 4
            for d in range(2):
                whole = dir_in.at[r, d, k]
                remote(
                    whole.at[pl.ds((1 - d) * HALF, HALF)], whole.at[pl.ds((1 - d) * HALF, HALF)],
                    dirs, (r, d, k), xdev[d],
                ).wait_recv()
                remote(acc.at[r, d, k], whole.at[pl.ds(d * HALF, HALF)], accs, (r, d, k), xdev[d]).wait_recv()
            xsum[r, k] = part[r, rows(x * CHUNK + k * SUB, SUB), :] + dir_in[r, 0, k] + dir_in[r, 1, k]
            if j:
                go(xsum.at[r, k], z_in.at[r, j - 1], zs, (r, j - 1), at_aux(x, z + j))

    def amplitude(r):
        total = xsum[r, z]
        for j in (1, 2, 3):
            remote(z_in.at[r, j - 1], z_in.at[r, j - 1], zs, (r, j - 1), at_aux(x, z + j)).wait_recv()
            total = total + z_in[r, j - 1]
        energy = occ[own_slot(r)] + peer[r, V : V + 1, 0:1]
        mine = rows(a * SUB, SUB)
        lane = lax.broadcasted_iota(jnp.int32, (SUB, V), 1)
        line = lax.broadcasted_iota(jnp.int32, (SUB, V), 0) + a * SUB
        across_v = virt[...].reshape(1, V)
        level = jnp.sum(jnp.where(lane == line, across_v, 0.0), axis=1, keepdims=True)
        full[r, mine, :] = total / ((energy - level) - across_v)

    def block(r, xx, zz):
        return full.at[r, rows((xx % 4) * CHUNK + (zz % 4) * SUB, SUB)]

    def piece(r, xx, zz, d):
        return full.at[r, rows((xx % 4) * CHUNK + (zz % 4) * SUB + d * HALF, HALF)]

    def ring_block(r, d, k):
        return remote(block(r, x, k), block(r, x, k), agx, (r, d, k), xdev[d])

    def straight(r, j):
        mine = block(r, x, z)
        return remote(mine, mine, agd, (r, j - 1), at_aux(x, z + j))

    def gather_z(r):
        for j in (1, 3, 2):
            straight(r, j).start()

    def gather_x(r):
        for d in range(2):
            ring_block(r, d, z).start()

    def onward(r, *which):
        for i in which:
            k = (z - i + 4) % 4
            got = block(r, x, k)
            remote(got, got, agd, (r, i - 1), at_aux(x, z + i)).wait_recv()
            for e in range(2):
                ring_block(r, e, k).start()

    def ring_relay(r, d, k):
        on = piece(r, x + 3 - 2 * d, k, d)
        return remote(on, on, rel, (r, d, k), xdev[d])

    def relay(r, *which):
        for i in which:
            k = (z - i + 4) % 4
            for d in range(2):
                got = block(r, x + 3 - 2 * d, k)
                remote(got, got, agx, (r, d, k), xdev[d]).wait_recv()
                ring_relay(r, d, k).start()

    def arrived(r):
        for j in (0, 1, 3, 2):
            k = (z - j + 4) % 4
            for d in range(2):
                got = piece(r, x + 2, k, d)
                remote(got, got, rel, (r, d, k), xdev[d]).wait_recv()

    def tildes(r):
        def step(i, carry):
            at = pl.ds(pl.multiple_of(i * 128, 128), 128)
            here = full[r, at, :]
            there = full[r, :, at].T
            th[at, :], tl[at, :] = split(2.0 * there - here)
            uh[at, :], ul[at, :] = split(2.0 * here - there)
            return carry

        lax.fori_loop(0, V // 128, step, 0)

    def give_back(r, first=0, last=TILES):
        o = own_slot(r)
        for i in range(first, last):
            at = pl.ds(i * CHUNK, CHUNK)
            rsend[r, at, :] = dot3((uh[at, :], ul[at, :]), (bh[o], bl[o]), NN)
            go(rsend.at[r, at], rrecv.at[r, at], ret, (r, i), partner(r))

    def keep(r):
        def step(i, carry):
            at = rows(i * CHUNK, CHUNK)
            gown[r, at, :] = dot3((th[at, :], tl[at, :]), (ph[r], plo[r]), NN)
            return carry

        lax.fori_loop(0, TILES, step, 0)

    def density(r, first=False):
        mine = rows(a * SUB, SUB)
        amp = full[r, mine, :]
        amp_t = 2.0 * amp - (uh[mine, :].astype(F32) + ul[mine, :].astype(F32))
        pad = jnp.zeros((128 - SUB, V), F32)
        amp = split(jnp.concatenate([amp, pad], axis=0))
        amp_t = split(jnp.concatenate([amp_t, pad], axis=0))

        for i in range(TILES):
            at = pl.ds(i * CHUNK, CHUNK)
            value = dot3((uh[at, :], ul[at, :]), amp, NT) + dot3((th[at, :], tl[at, :]), amp_t, NT)
            value = value.reshape(2, 2, SUB, 128)
            if first:
                dt[2 * i : 2 * i + 2] = value
            else:
                dt[2 * i : 2 * i + 2] = dt[2 * i : 2 * i + 2] + value

    def column_copies():
        return [remote(s2.at[(y + j) % 4], d3.at[j - 1], dsem, (1 + j,), at_pair(zh, y + j, core)) for j in (1, 2, 3)]

    def chip_copy():
        return remote(dt.at[:, 1 - core], d1, dsem, (0,), chip_mate)

    def far_copy():
        return remote(s1.at[pl.ds(4 * (1 - zh), 4)], d2, dsem, (1,), at_pair(1 - zh, y, core))

    def spread(stage):
        if stage == 0:
            chip_copy().start()
        if stage == 1:
            chip_copy().wait_recv()
            s1[...] = dt[:, core] + d1[...]
            far_copy().start()
        if stage == 2:
            far_copy().wait_recv()
            s2[...] = s1[pl.ds(4 * zh, 4)] + d2[...]
            for copy in column_copies():
                copy.start()

    def settle():
        total = s2[y]
        for j, copy in enumerate(column_copies()):
            copy.wait_recv()
            total = total + d3[j]
        total = jnp.concatenate([total, jnp.zeros((128 - SUB, 128), F32)], axis=0).T
        dens_out[...] = total[0:SUB, 0:SUB]
        sent.extend([chip_copy(), far_copy()] + column_copies())

    def finish():
        o0 = own_slot(0)
        o1 = own_slot(1)
        writes = []
        for i in range(TILES):
            at = pl.ds(i * CHUNK, CHUNK)
            for r in range(2):
                remote(rsend.at[r, at], rrecv.at[r, at], ret, (r, i), partner(r)).wait_recv()
            k0, k1, n0, n1 = gown[0, at, :], gown[1, at, :], rrecv[0, at, :], rrecv[1, at, :]
            gown[0, at, :] = jnp.where(o0 == 0, k0, n0) + jnp.where(o1 == 0, k1, n1)
            gown[1, at, :] = jnp.where(o0 == 0, n0, k0) + jnp.where(o1 == 0, n1, k1)
            copy = pltpu.make_async_copy(gown.at[:, at], grad_hbm.at[:, at], outs.at[i])
            copy.start()
            writes.append(copy)
        settle()
        for r in range(2):
            for i in range(5):
                row_chunk(r, i).wait_send()
        for copy in sent:
            copy.wait_send()
        for r in range(2):
            for j in (1, 2, 3):
                straight(r, j).wait_send()
            for k in range(4):
                for d in range(2):
                    ring_block(r, d, k).wait_send()
                    ring_relay(r, d, k).wait_send()
        for copy in writes:
            copy.wait()

    lax.fori_loop(0, TILES, split_own, 0)
    before = list(sent)

    @pl.when(core == 0)
    def _():
        sent[:] = before
        integral(0, 0, 1)
        integral(1, 0)
        integral(0, 2, 3)
        integral(1, 1, 2)
        pass_on(1)
        integral(1, 3)
        pass_on(0)
        across(1)
        amplitude(1)
        gather_z(1)
        gather_x(1)
        across(0)
        onward(1, 1)
        relay(1, 0)
        onward(1, 3)
        relay(1, 1)
        onward(1, 2)
        relay(1, 3)
        relay(1, 2)
        amplitude(0)
        arrived(1)
        tildes(1)
        give_back(1)
        gather_z(0)
        gather_x(0)
        keep(1)
        density(1, True)
        onward(0, 1, 3, 2)
        relay(0, 0)
        relay(0, 1)
        relay(0, 3, 2)
        arrived(0)
        tildes(0)
        density(0)
        spread(0)
        give_back(0)
        spread(1)
        keep(0)
        spread(2)
        finish()

    @pl.when(core == 1)
    def _():
        sent[:] = before
        integral(0, 0, 1, 2, 3)
        pass_on(0)
        exchange(1)
        across(0)
        integral(1, 0)
        amplitude(0)
        gather_x(0)
        integral(1, 1, 2)
        pass_on(1)
        integral(1, 3)
        across(1)
        amplitude(1)
        gather_z(1)
        gather_x(1)
        gather_z(0)
        onward(1, 1)
        relay(1, 0)
        onward(1, 3)
        relay(1, 1)
        onward(1, 2)
        relay(1, 3, 2)
        relay(0, 0)
        arrived(1)
        tildes(1)
        give_back(1)
        onward(0, 1, 3, 2)
        relay(0, 1)
        keep(1)
        relay(0, 3, 2)
        density(1, True)
        arrived(0)
        tildes(0)
        density(0)
        spread(0)
        give_back(0, 0, 2)
        spread(1)
        give_back(0, 2, 4)
        keep(0)
        spread(2)
        finish()


def body(three_index, occupied_energy, virtual_energy, plan):
    vm = pltpu.VMEM
    dma = pltpu.SemaphoreType.DMA
    return pl.pallas_call(
        kernel,
        out_shape=(
            jax.ShapeDtypeStruct((2, V, NP), F32),
            jax.ShapeDtypeStruct((SUB, SUB), F32),
        ),
        in_specs=[
            pl.BlockSpec(memory_space=pl.ANY),
            pl.BlockSpec(memory_space=pltpu.SMEM),
            pl.BlockSpec(memory_space=pltpu.SMEM),
            pl.BlockSpec(memory_space=pltpu.VMEM),
        ],
        out_specs=(pl.BlockSpec(memory_space=pl.ANY), pl.BlockSpec(memory_space=pltpu.VMEM)),
        scratch_shapes=[
            vm((2, V, NP), F32),
            vm((2, V, NP), BF16),
            vm((2, V, NP), BF16),
            vm((2, V + 8, NP), F32),
            vm((2, V + 8, NP), F32),
            vm((2, V, NP), BF16),
            vm((2, V, NP), BF16),
            vm((2, V, V), F32),
            vm((2, 2, 4, HALF, V), F32),
            vm((2, 2, 4, SUB, V), F32),
            vm((2, 2, 4, HALF, V), F32),
            vm((2, 4, SUB, V), F32),
            vm((2, 3, SUB, V), F32),
            vm((2, V, V), F32),
            vm((V, V), BF16),
            vm((V, V), BF16),
            vm((V, V), BF16),
            vm((V, V), BF16),
            vm((2, V, NP), F32),
            vm((2, V, NP), F32),
            vm((2, V, NP), F32),
            vm((8, 2, SUB, 128), F32),
            vm((8, SUB, 128), F32),
            vm((8, SUB, 128), F32),
            vm((4, SUB, 128), F32),
            vm((4, SUB, 128), F32),
            vm((3, SUB, 128), F32),
            dma,
            dma((2, 2, 5)),
            dma((2, 2, 2, 4)),
            dma((2, 2, 2, 4)),
            dma((2, 2, 2, 4)),
            dma((2, 2, 3)),
            dma((2, 2, 3)),
            dma((2, 2, 2, 4)),
            dma((2, 2, 2, 4)),
            dma((2, 2, TILES)),
            dma((2, 5)),
            dma((TILES,)),
        ],
        compiler_params=pltpu.CompilerParams(
            collective_id=0, has_side_effects=True, vmem_limit_bytes=50 * 1024 * 1024
        ),
        name="pairs",
    )(three_index, occupied_energy, plan, virtual_energy)


def solution(mesh):
    in_specs = (P("pair", None, "aux"), P("pair"), P(), P(None, "pair"))
    out_specs = (P("pair", None, "aux"), P("aux", "pair"))
    return jax.shard_map(body, mesh=mesh, in_specs=in_specs, out_specs=out_specs, check_vma=False)
```

```python
import functools

import jax
import jax.numpy as jnp
from jax import lax
from jax.experimental import pallas as pl
from jax.experimental.pallas import tpu as pltpu
from jax.sharding import PartitionSpec as P

MESH = pl.DeviceIdType.MESH
F32 = jnp.float32
BF16 = jnp.bfloat16
V = 768
NP = 512
SUB = 48
HALF = SUB // 2
CHUNK = 4 * SUB
TILES = V // CHUNK
NN = (((1,), (0,)), ((), ()))
NT = (((1,), (1,)), ((), ()))


def split(value):
    high = value.astype(BF16)
    return high, (value - high.astype(F32)).astype(BF16)


def dot3(left, right, dims):
    (lh, ll), (rh, rl) = left, right

    def one(x, y):
        return lax.dot_general(x, y, dims, preferred_element_type=F32)

    return one(lh, rh) + (one(lh, rl) + one(ll, rh))


def rows(start, count):
    return pl.ds(pl.multiple_of(start, 8), count)


def kernel(
    b_hbm, occ, plan, virt, grad_hbm, dens_out,
    blk, bh, bl, sendb, peer, ph, plo, part, far_in, dir_in, acc, xsum, z_in, full, th, tl, uh, ul,
    rsend, rrecv, gown, dt, d1, s1, d2, s2, d3,
    ld, ex, far, dirs, accs, zs, agd, agx, rel, ret, dsem, outs,
):
    p = lax.axis_index("pair")
    a = lax.axis_index("aux")
    core = p % 2
    y = (p // 2) % 4
    zh = p // 8
    x = a // 4
    z = a % 4

    def at_aux(xx, zz):
        return (p, (xx % 4) * 4 + zz % 4)

    def at_pair(hh, yy, cc):
        return (hh * 8 + (yy % 4) * 2 + cc, a)

    xdev = (at_aux(x + 1, z), at_aux(x + 3, z))
    chip_mate = at_pair(zh, y, 1 - core)
    y_mate = at_pair(zh, y + 1 - 2 * (y % 2), core)
    load = pltpu.make_async_copy(b_hbm, blk, ld)
    load.start()

    barrier = pltpu.get_barrier_semaphore()
    friends = [xdev[0], xdev[1], chip_mate, at_pair(1 - zh, y, core)]
    friends += [at_aux(x, z + j) for j in (1, 2, 3)]
    friends += [at_pair(zh, y + j, core) for j in (1, 2, 3)]
    for dev in friends:
        pl.semaphore_signal(barrier, inc=1, device_id=dev, device_id_type=MESH)

    def remote(src, dst, sems, index, dev):
        return pltpu.make_async_remote_copy(
            src_ref=src,
            dst_ref=dst,
            send_sem=sems.at[(0,) + index],
            recv_sem=sems.at[(1,) + index],
            device_id=dev,
            device_id_type=MESH,
        )

    sent = []

    def go(*args):
        copy = remote(*args)
        copy.start()
        sent.append(copy)

    def upper(r):
        return core + r * (y % 2 - core)

    def own_slot(r):
        return upper(r) * (1 - plan[r, 0])

    def partner(r):
        return (p + (1 + r) * (1 - 2 * upper(r)), a)

    load.wait()

    def fill(r):
        other = 1 - own_slot(r)
        sendb[r, 0:V, :] = blk[other]
        sendb[r, V : V + 8, :] = jnp.full((8, NP), occ[other], F32)

    chunks = (2, 1, 3, 0)

    def row_chunk(r, i):
        at = rows(((x + chunks[i]) % 4) * CHUNK, CHUNK) if i < 4 else pl.ds(V, 8)
        return remote(sendb.at[r, at], peer.at[r, at], ex, (r, i), partner(r))

    def exchange(r):
        for i in (4, 0, 1, 2, 3):
            row_chunk(r, i).start()

    fill(0)
    fill(1)
    pl.semaphore_wait(barrier, len(friends))

    @pl.when(core == 0)
    def _():
        exchange(1)

    exchange(0)

    def split_own(i, carry):
        at = rows(i * CHUNK, CHUNK)
        for slot in range(2):
            high, low = split(blk[slot, at, :])
            bh[slot, at, :] = high
            bl[slot, at, :] = low
        return carry

    order = (2, 3, 1, 0)

    def integral(r, *which):
        for i in which:
            if i == 0:
                row_chunk(r, 4).wait_recv()
            row_chunk(r, i).wait_recv()
            c = (x + chunks[i]) % 4
            at = rows(c * CHUNK, CHUNK)
            o = own_slot(r)
            high, low = split(peer[r, at, :])
            ph[r, at, :] = high
            plo[r, at, :] = low
            part[r, at, :] = dot3((high, low), (bh[o], bl[o]), NT)
            for j in order:
                k = (z + j) % 4
                base = c * CHUNK + k * SUB
                if i == 0:
                    for d in range(2):
                        go(part.at[r, rows(base + d * HALF, HALF)], far_in.at[r, d, k], far, (r, d, k), xdev[d])
                elif i < 3:
                    d = i - 1
                    go(
                        part.at[r, rows(base + (1 - d) * HALF, HALF)],
                        dir_in.at[r, d, k, pl.ds((1 - d) * HALF, HALF)],
                        dirs, (r, d, k), xdev[d],
                    )

    def pass_on(r):
        for j in order:
            k = (z + j) % 4
            for d in range(2):
                remote(far_in.at[r, d, k], far_in.at[r, d, k], far, (r, d, k), xdev[d]).wait_recv()
                base = ((x + 1 + 2 * d) % 4) * CHUNK + k * SUB + d * HALF
                acc[r, d, k] = part[r, rows(base, HALF), :] + far_in[r, d, k]
                go(acc.at[r, d, k], dir_in.at[r, d, k, pl.ds(d * HALF, HALF)], accs, (r, d, k), xdev[d])

    def across(r):
        for j in order:
            k = (z + j) % 4
            for d in range(2):
                whole = dir_in.at[r, d, k]
                remote(
                    whole.at[pl.ds((1 - d) * HALF, HALF)], whole.at[pl.ds((1 - d) * HALF, HALF)],
                    dirs, (r, d, k), xdev[d],
                ).wait_recv()
                remote(acc.at[r, d, k], whole.at[pl.ds(d * HALF, HALF)], accs, (r, d, k), xdev[d]).wait_recv()
            xsum[r, k] = part[r, rows(x * CHUNK + k * SUB, SUB), :] + dir_in[r, 0, k] + dir_in[r, 1, k]
            if j:
                go(xsum.at[r, k], z_in.at[r, j - 1], zs, (r, j - 1), at_aux(x, z + j))

    def amplitude(r):
        total = xsum[r, z]
        for j in (1, 2, 3):
            remote(z_in.at[r, j - 1], z_in.at[r, j - 1], zs, (r, j - 1), at_aux(x, z + j)).wait_recv()
            total = total + z_in[r, j - 1]
        energy = occ[own_slot(r)] + peer[r, V : V + 1, 0:1]
        mine = rows(a * SUB, SUB)
        lane = lax.broadcasted_iota(jnp.int32, (SUB, V), 1)
        line = lax.broadcasted_iota(jnp.int32, (SUB, V), 0) + a * SUB
        across_v = virt[...].reshape(1, V)
        level = jnp.sum(jnp.where(lane == line, across_v, 0.0), axis=1, keepdims=True)
        full[r, mine, :] = total / ((energy - level) - across_v)

    def block(r, xx, zz):
        return full.at[r, rows((xx % 4) * CHUNK + (zz % 4) * SUB, SUB)]

    def piece(r, xx, zz, d):
        return full.at[r, rows((xx % 4) * CHUNK + (zz % 4) * SUB + d * HALF, HALF)]

    def ring_block(r, d, k):
        return remote(block(r, x, k), block(r, x, k), agx, (r, d, k), xdev[d])

    def straight(r, j):
        mine = block(r, x, z)
        return remote(mine, mine, agd, (r, j - 1), at_aux(x, z + j))

    def gather_z(r):
        for j in (1, 3, 2):
            straight(r, j).start()

    def gather_x(r):
        for d in range(2):
            ring_block(r, d, z).start()

    def onward(r, *which):
        for i in which:
            k = (z - i + 4) % 4
            got = block(r, x, k)
            remote(got, got, agd, (r, i - 1), at_aux(x, z + i)).wait_recv()
            for e in range(2):
                ring_block(r, e, k).start()

    def ring_relay(r, d, k):
        on = piece(r, x + 3 - 2 * d, k, d)
        return remote(on, on, rel, (r, d, k), xdev[d])

    def relay(r, *which):
        for i in which:
            k = (z - i + 4) % 4
            for d in range(2):
                got = block(r, x + 3 - 2 * d, k)
                remote(got, got, agx, (r, d, k), xdev[d]).wait_recv()
                ring_relay(r, d, k).start()

    def arrived(r):
        for j in (0, 1, 3, 2):
            k = (z - j + 4) % 4
            for d in range(2):
                got = piece(r, x + 2, k, d)
                remote(got, got, rel, (r, d, k), xdev[d]).wait_recv()

    def tildes(r):
        def step(i, carry):
            at = pl.ds(pl.multiple_of(i * 128, 128), 128)
            here = full[r, at, :]
            there = full[r, :, at].T
            th[at, :], tl[at, :] = split(2.0 * there - here)
            uh[at, :], ul[at, :] = split(2.0 * here - there)
            return carry

        lax.fori_loop(0, V // 128, step, 0)

    def give_back(r, first=0, last=TILES):
        o = own_slot(r)
        for i in range(first, last):
            at = pl.ds(i * CHUNK, CHUNK)
            rsend[r, at, :] = dot3((uh[at, :], ul[at, :]), (bh[o], bl[o]), NN)
            go(rsend.at[r, at], rrecv.at[r, at], ret, (r, i), partner(r))

    def keep(r):
        def step(i, carry):
            at = rows(i * CHUNK, CHUNK)
            gown[r, at, :] = dot3((th[at, :], tl[at, :]), (ph[r], plo[r]), NN)
            return carry

        lax.fori_loop(0, TILES, step, 0)

    def density(r, first=False):
        mine = rows(a * SUB, SUB)
        amp = full[r, mine, :]
        amp_t = 2.0 * amp - (uh[mine, :].astype(F32) + ul[mine, :].astype(F32))
        pad = jnp.zeros((128 - SUB, V), F32)
        amp = split(jnp.concatenate([amp, pad], axis=0))
        amp_t = split(jnp.concatenate([amp_t, pad], axis=0))

        for i in range(TILES):
            at = pl.ds(i * CHUNK, CHUNK)
            value = dot3((uh[at, :], ul[at, :]), amp, NT) + dot3((th[at, :], tl[at, :]), amp_t, NT)
            value = value.reshape(2, 2, SUB, 128)
            if first:
                dt[2 * i : 2 * i + 2] = value
            else:
                dt[2 * i : 2 * i + 2] = dt[2 * i : 2 * i + 2] + value

    def column_copies():
        return [remote(s2.at[(y + j) % 4], d3.at[j - 1], dsem, (1 + j,), at_pair(zh, y + j, core)) for j in (1, 2, 3)]

    def chip_copy():
        return remote(dt.at[:, 1 - core], d1, dsem, (0,), chip_mate)

    def far_copy():
        return remote(s1.at[pl.ds(4 * (1 - zh), 4)], d2, dsem, (1,), at_pair(1 - zh, y, core))

    def spread(stage):
        if stage == 0:
            chip_copy().start()
        if stage == 1:
            chip_copy().wait_recv()
            s1[...] = dt[:, core] + d1[...]
            far_copy().start()
        if stage == 2:
            far_copy().wait_recv()
            s2[...] = s1[pl.ds(4 * zh, 4)] + d2[...]
            for copy in column_copies():
                copy.start()

    def settle():
        total = s2[y]
        for j, copy in enumerate(column_copies()):
            copy.wait_recv()
            total = total + d3[j]
        total = jnp.concatenate([total, jnp.zeros((128 - SUB, 128), F32)], axis=0).T
        dens_out[...] = total[0:SUB, 0:SUB]
        sent.extend([chip_copy(), far_copy()] + column_copies())

    def finish():
        o0 = own_slot(0)
        o1 = own_slot(1)
        writes = []
        for i in range(TILES):
            at = pl.ds(i * CHUNK, CHUNK)
            for r in range(2):
                remote(rsend.at[r, at], rrecv.at[r, at], ret, (r, i), partner(r)).wait_recv()
            k0, k1, n0, n1 = gown[0, at, :], gown[1, at, :], rrecv[0, at, :], rrecv[1, at, :]
            gown[0, at, :] = jnp.where(o0 == 0, k0, n0) + jnp.where(o1 == 0, k1, n1)
            gown[1, at, :] = jnp.where(o0 == 0, n0, k0) + jnp.where(o1 == 0, n1, k1)
            copy = pltpu.make_async_copy(gown.at[:, at], grad_hbm.at[:, at], outs.at[i])
            copy.start()
            writes.append(copy)
        settle()
        for r in range(2):
            for i in range(5):
                row_chunk(r, i).wait_send()
        for copy in sent:
            copy.wait_send()
        for r in range(2):
            for j in (1, 2, 3):
                straight(r, j).wait_send()
            for k in range(4):
                for d in range(2):
                    ring_block(r, d, k).wait_send()
                    ring_relay(r, d, k).wait_send()
        for copy in writes:
            copy.wait()

    lax.fori_loop(0, TILES, split_own, 0)
    before = list(sent)

    @pl.when(core == 0)
    def _():
        sent[:] = before
        integral(0, 0, 1)
        integral(1, 0)
        integral(0, 2, 3)
        integral(1, 1, 2)
        pass_on(1)
        integral(1, 3)
        pass_on(0)
        across(1)
        amplitude(1)
        gather_z(1)
        gather_x(1)
        across(0)
        onward(1, 1)
        relay(1, 0)
        onward(1, 3)
        relay(1, 1)
        onward(1, 2)
        amplitude(0)
        gather_z(0)
        relay(1, 3)
        relay(1, 2)
        gather_x(0)
        arrived(1)
        tildes(1)
        give_back(1)
        onward(0, 1, 3, 2)
        keep(1)
        relay(0, 0)
        density(1, True)
        relay(0, 1)
        relay(0, 3, 2)
        arrived(0)
        tildes(0)
        density(0)
        spread(0)
        give_back(0)
        spread(1)
        keep(0)
        spread(2)
        finish()

    @pl.when(core == 1)
    def _():
        sent[:] = before
        integral(0, 0, 1, 2, 3)
        pass_on(0)
        exchange(1)
        across(0)
        integral(1, 0)
        amplitude(0)
        gather_x(0)
        integral(1, 1, 2)
        pass_on(1)
        integral(1, 3)
        across(1)
        amplitude(1)
        gather_z(1)
        gather_x(1)
        gather_z(0)
        onward(1, 1)
        relay(1, 0)
        onward(1, 3)
        relay(1, 1)
        onward(1, 2)
        relay(1, 3, 2)
        relay(0, 0)
        onward(0, 1)
        arrived(1)
        tildes(1)
        give_back(1)
        onward(0, 3, 2)
        relay(0, 1)
        keep(1)
        relay(0, 3, 2)
        density(1, True)
        arrived(0)
        tildes(0)
        density(0)
        spread(0)
        give_back(0, 0, 2)
        spread(1)
        give_back(0, 2, 4)
        keep(0)
        spread(2)
        finish()


def body(three_index, occupied_energy, virtual_energy, plan):
    vm = pltpu.VMEM
    dma = pltpu.SemaphoreType.DMA
    return pl.pallas_call(
        kernel,
        out_shape=(
            jax.ShapeDtypeStruct((2, V, NP), F32),
            jax.ShapeDtypeStruct((SUB, SUB), F32),
        ),
        in_specs=[
            pl.BlockSpec(memory_space=pl.ANY),
            pl.BlockSpec(memory_space=pltpu.SMEM),
            pl.BlockSpec(memory_space=pltpu.SMEM),
            pl.BlockSpec(memory_space=pltpu.VMEM),
        ],
        out_specs=(pl.BlockSpec(memory_space=pl.ANY), pl.BlockSpec(memory_space=pltpu.VMEM)),
        scratch_shapes=[
            vm((2, V, NP), F32),
            vm((2, V, NP), BF16),
            vm((2, V, NP), BF16),
            vm((2, V + 8, NP), F32),
            vm((2, V + 8, NP), F32),
            vm((2, V, NP), BF16),
            vm((2, V, NP), BF16),
            vm((2, V, V), F32),
            vm((2, 2, 4, HALF, V), F32),
            vm((2, 2, 4, SUB, V), F32),
            vm((2, 2, 4, HALF, V), F32),
            vm((2, 4, SUB, V), F32),
            vm((2, 3, SUB, V), F32),
            vm((2, V, V), F32),
            vm((V, V), BF16),
            vm((V, V), BF16),
            vm((V, V), BF16),
            vm((V, V), BF16),
            vm((2, V, NP), F32),
            vm((2, V, NP), F32),
            vm((2, V, NP), F32),
            vm((8, 2, SUB, 128), F32),
            vm((8, SUB, 128), F32),
            vm((8, SUB, 128), F32),
            vm((4, SUB, 128), F32),
            vm((4, SUB, 128), F32),
            vm((3, SUB, 128), F32),
            dma,
            dma((2, 2, 5)),
            dma((2, 2, 2, 4)),
            dma((2, 2, 2, 4)),
            dma((2, 2, 2, 4)),
            dma((2, 2, 3)),
            dma((2, 2, 3)),
            dma((2, 2, 2, 4)),
            dma((2, 2, 2, 4)),
            dma((2, 2, TILES)),
            dma((2, 5)),
            dma((TILES,)),
        ],
        compiler_params=pltpu.CompilerParams(
            collective_id=0, has_side_effects=True, vmem_limit_bytes=50 * 1024 * 1024
        ),
        name="pairs",
    )(three_index, occupied_energy, plan, virtual_energy)


def solution(mesh):
    in_specs = (P("pair", None, "aux"), P("pair"), P(), P(None, "pair"))
    out_specs = (P("pair", None, "aux"), P("aux", "pair"))
    return jax.shard_map(body, mesh=mesh, in_specs=in_specs, out_specs=out_specs, check_vma=False)
```
